32 devices in a mesh: dev: 32 (over z, y, x, core).
Axes of the slice: x: 2, y: 2, z: 4, core: 2. Of those that a mesh axis runs over, the one named last changes fastest.
Arguments:
- tensor_tiles: bfloat16 [128, 64, 128, 128], P('dev'), may hold values from -196608 to 196608
- tile_coords: int32 [128, 3], P('dev'), may hold values from 0 to 31, as said below
- tile_count: int32 [32], P('dev'), may hold values from 1 to 4, as said below
- owned_i: int32 [32], P('dev'), may hold values from 0 to 31, as said below
- owned_j: int32 [32], P('dev'), may hold values from 0 to 31, as said below
- owned_k: int32 [32], P('dev'), may hold values from 0 to 31, as said below
- factor_a: float32 [32, 64, 512], P('dev'), may hold values from 0 to 7
- factor_b: float32 [32, 128, 512], P('dev'), may hold values from 0 to 7
- factor_c: float32 [32, 128, 512], P('dev'), may hold values from 0 to 7
- dual_a: float32 [32, 64, 512], P('dev'), may hold values from -1.75 to 1.75
- dual_b: float32 [32, 128, 512], P('dev'), may hold values from -1.75 to 1.75
- dual_c: float32 [32, 128, 512], P('dev'), may hold values from -1.75 to 1.75
- penalty: float32 [3], replicated, may hold values from 0.5 to 2
Outputs:
- factor_a_new: float32 [32, 64, 512], P('dev')
- dual_a_new: float32 [32, 64, 512], P('dev')
- factor_b_new: float32 [32, 128, 512], P('dev')
- dual_b_new: float32 [32, 128, 512], P('dev')
- factor_c_new: float32 [32, 128, 512], P('dev')
- dual_c_new: float32 [32, 128, 512], P('dev')
The draws below stay inside these ranges and needn't reach their ends.
Inputs may be any that keep to these rules, and one draw needn't show every extreme that they name: `owned_i`: each block number appears once. `owned_j`: each block number appears once. `owned_k`: each block number appears once. `tile_coords`: for a live slot on device d, the block named for each mode is owned by a device d + o with o between -2 and 2, counted around the axis; slots may name the same blocks, and their tiles then add; slots that are not live hold arbitrary block numbers. `tile_count`: some device has all 4 slots live.
All inputs are finite; a program needn't handle non-finite values.
Results may differ from the reference program's by a relative error of at most 0.0025.
The reference program's roundings to bfloat16 on the way count: a program that leaves them out, or rounds other values in their place, can miss the bound.
Values may be sent and summed in bfloat16 or wider, within the bound.
A program may use at most 128 MiB of HBM per device.

```python
import math
import jax
import jax.numpy as jnp
from jax import lax

R = 512
TI = 64
TJ = 128
TK = 128
CAP = 4
ITERS = 6
REACH = 2
TILES = 128
N_DEV = 32


def layout(key):
    permutations = [jax.random.permutation(jax.random.fold_in(key, 1000 + mode_index), N_DEV).astype(jnp.int32) for mode_index in range(3)]
    level_draw = jax.random.randint(jax.random.fold_in(key, 1010), (N_DEV,), 0, 16)
    counts = 1 + (level_draw >= 8).astype(jnp.int32) + (level_draw >= 12).astype(jnp.int32) + (level_draw >= 14).astype(jnp.int32)
    counts = jnp.minimum(counts, CAP)
    busiest = jax.random.randint(jax.random.fold_in(key, 1011), (), 0, N_DEV)
    counts = jnp.where(jnp.arange(N_DEV) == busiest, CAP, counts).astype(jnp.int32)
    shifts = jax.random.randint(jax.random.fold_in(key, 1012), (N_DEV * CAP, 3), -REACH, REACH + 1)
    home_device = jnp.arange(N_DEV * CAP, dtype=jnp.int32) // CAP
    owner_device = (home_device[:, None] + shifts) % N_DEV
    coords = jnp.stack([permutations[mode_index][owner_device[:, mode_index]] for mode_index in range(3)], axis=1).astype(jnp.int32)
    return (permutations, counts, coords)


def draw_tile_coords(key, part):
    return layout(key)[2]


def draw_tile_count(key, part):
    return layout(key)[1]


def draw_owned_i(key, part):
    return layout(key)[0][0]


def draw_owned_j(key, part):
    return layout(key)[0][1]


def draw_owned_k(key, part):
    return layout(key)[0][2]


def factor_draw(key, salt_value, row_count):
    base_draw = jax.random.uniform(jax.random.fold_in(key, salt_value), (N_DEV, row_count, R), jnp.float32)
    rising = 0.6 + 1.2 * jnp.arange(N_DEV, dtype=jnp.float32) / (N_DEV - 1)
    column = jnp.exp(jax.random.uniform(jax.random.fold_in(key, salt_value + 1), (R,), jnp.float32, -0.7, 0.7))
    values_out = base_draw * rising[:, None, None] * column[None, None, :]
    return values_out


def draw_factor_a(key, part):
    return factor_draw(key, 2000, TI)


def draw_factor_b(key, part):
    return factor_draw(key, 3000, TJ)


def draw_factor_c(key, part):
    return factor_draw(key, 4000, TK)


def shard_levels(rng, dims, pieces, least, largest):
    def one(position, shards_of):
        heights = jax.random.uniform(jax.random.fold_in(jax.random.fold_in(rng, 6), position), (shards_of,), jnp.float32, least / len(pieces), largest / len(pieces))
        return jnp.repeat(jnp.exp(heights), dims[position] // shards_of).reshape((-1,) + (1,) * (len(dims) - position - 1))

    loudness = one(*pieces[0])
    for cut in pieces[1:]:
        loudness = loudness * one(*cut)
    return loudness


def noise(stream_key, shape, scale, reach, cuts=(), held_as=jnp.bfloat16):
    values = jax.random.normal(stream_key, shape, jnp.float32) * scale
    if len(cuts) > 0:
        values = shard_levels(stream_key, shape, cuts, -0.22, 0.18) * values
    return jnp.clip(values, min=-reach, max=reach).astype(held_as)


def setup_inputs(seed: int = 0) -> dict:
    key_of = jax.random.split(jax.random.key(seed), 14)
    tensor_tiles = noise(key_of[0], (TILES, TI, TJ, TK), (TJ * N_DEV * N_DEV // 4), 196608.0, ((0, 32),))
    tile_coords = draw_tile_coords(jax.random.fold_in(key_of[13], 71), 0)
    tile_count = draw_tile_count(jax.random.fold_in(key_of[13], 71), 0)
    owned_i = draw_owned_i(jax.random.fold_in(key_of[13], 71), 0)
    owned_j = draw_owned_j(jax.random.fold_in(key_of[13], 71), 0)
    owned_k = draw_owned_k(jax.random.fold_in(key_of[13], 71), 0)
    factor_a = draw_factor_a(jax.random.fold_in(key_of[13], 71), 0)
    factor_b = draw_factor_b(jax.random.fold_in(key_of[13], 71), 0)
    factor_c = draw_factor_c(jax.random.fold_in(key_of[13], 71), 0)
    dual_a = noise(key_of[9], (N_DEV, TI, R), 0.3, 1.75, ((0, 32),), jnp.float32)
    dual_b = noise(key_of[10], (N_DEV, TJ, R), 0.3, 1.75, ((0, 32),), jnp.float32)
    dual_c = noise(key_of[11], (N_DEV, TK, R), 0.3, 1.75, ((0, 32),), jnp.float32)
    penalty = jnp.clip(jnp.exp(jax.random.uniform(key_of[12], (3,), jnp.float32, math.log(0.5), math.log(2.0))), 0.5, 2.0)
    return dict(tensor_tiles=tensor_tiles, tile_coords=tile_coords, tile_count=tile_count, owned_i=owned_i, owned_j=owned_j, owned_k=owned_k, factor_a=factor_a, factor_b=factor_b, factor_c=factor_c, dual_a=dual_a, dual_b=dual_b, dual_c=dual_c, penalty=penalty)


def chol_solve(chol_low, right_side):
    middle = lax.linalg.triangular_solve(chol_low, right_side, left_side=True, lower=True)
    return lax.linalg.triangular_solve(chol_low, middle, left_side=True, lower=True, transpose_a=True)

def gram_local(factor):
    flat_rows = factor.reshape(-1, factor.shape[-1])
    return jnp.dot(flat_rows.T, flat_rows, precision=lax.Precision.HIGHEST)

def place_rows(stored, owned):
    return jnp.zeros_like(stored).at[owned].set(stored)

def admm_update(mttkrp, factor, dual_var, gram_mat, weight):
    rank_size = gram_mat.shape[0]
    full_shape = factor.shape
    mttkrp = mttkrp.reshape(-1, rank_size)
    factor = factor.reshape(-1, rank_size)
    dual_var = dual_var.reshape(-1, rank_size)
    rho_value = weight * jnp.trace(gram_mat) / rank_size
    identity = jnp.eye(rank_size, dtype=jnp.float32)
    chol_low = jnp.linalg.cholesky(gram_mat + rho_value * identity)
    inverse = chol_solve(chol_low, identity)
    for sweep_index in range(ITERS):
        auxiliary = jnp.dot(mttkrp + rho_value * (factor + dual_var), inverse, precision=lax.Precision.HIGHEST)
        factor = jnp.maximum(auxiliary - dual_var, 0.0)
        dual_var = dual_var + factor - auxiliary
    return (factor.reshape(full_shape), dual_var.reshape(full_shape))

def accumulate(mode_index, tensor_tiles, tile_coords, live, first_glob, second_glob, blocks_zero):

    def keep_same(totals):
        return totals

    def scan_step(totals, item_now):
        tile_now, coord_row, alive = item_now

        def add_term(totals):
            tile_wide = tile_now.astype(jnp.float32)
            rows_first, rows_second, rows_third = tile_wide.shape
            if mode_index < 2:
                flat_tile = tile_wide.reshape(rows_first * rows_second, rows_third)
                partial_value = jnp.dot(flat_tile, second_glob[coord_row[2]].astype(jnp.float32), precision=lax.Precision.HIGHEST)
                partial_value = partial_value.reshape(rows_first, rows_second, -1)
                if mode_index == 0:
                    contrib = jnp.sum(partial_value * first_glob[coord_row[1]].astype(jnp.float32)[None, :, :], axis=1)
                else:
                    contrib = jnp.sum(partial_value * first_glob[coord_row[0]].astype(jnp.float32)[:, None, :], axis=0)
            else:
                flat_tile = tile_wide.reshape(rows_first, rows_second * rows_third)
                crossed = jnp.dot(flat_tile.T, first_glob[coord_row[0]].astype(jnp.float32), precision=lax.Precision.HIGHEST)
                crossed = crossed.reshape(rows_second, rows_third, -1)
                contrib = jnp.sum(crossed * second_glob[coord_row[1]].astype(jnp.float32)[:, None, :], axis=0)
            return totals.at[coord_row[mode_index]].add(contrib)
        return (lax.cond(alive, add_term, keep_same, totals), None)
    result, unused = lax.scan(scan_step, blocks_zero, (tensor_tiles, tile_coords, live))
    return result

def reference(tensor_tiles, tile_coords, tile_count, owned_i, owned_j, owned_k, factor_a, factor_b, factor_c, dual_a, dual_b, dual_c, penalty):
    slot_ids = jnp.arange(tensor_tiles.shape[0], dtype=jnp.int32)
    per_device = tensor_tiles.shape[0] // tile_count.shape[0]
    live = slot_ids % per_device < tile_count[slot_ids // per_device]
    gram_b = gram_local(factor_b)
    gram_c = gram_local(factor_c)
    glob_b = place_rows(factor_b, owned_j).astype(jnp.bfloat16)
    glob_c = place_rows(factor_c, owned_k).astype(jnp.bfloat16)
    mttkrp_a = accumulate(0, tensor_tiles, tile_coords, live, glob_b, glob_c, jnp.zeros(factor_a.shape, jnp.float32))[owned_i]
    factor_a_new, dual_a_new = admm_update(mttkrp_a, factor_a, dual_a, gram_b * gram_c, penalty[0])
    gram_a = gram_local(factor_a_new)
    glob_a = place_rows(factor_a_new, owned_i).astype(jnp.bfloat16)
    mttkrp_b = accumulate(1, tensor_tiles, tile_coords, live, glob_a, glob_c, jnp.zeros(factor_b.shape, jnp.float32))[owned_j]
    factor_b_new, dual_b_new = admm_update(mttkrp_b, factor_b, dual_b, gram_a * gram_c, penalty[1])
    gram_bn = gram_local(factor_b_new)
    glob_bn = place_rows(factor_b_new, owned_j).astype(jnp.bfloat16)
    mttkrp_c = accumulate(2, tensor_tiles, tile_coords, live, glob_a, glob_bn, jnp.zeros(factor_c.shape, jnp.float32))[owned_k]
    factor_c_new, dual_c_new = admm_update(mttkrp_c, factor_c, dual_c, gram_a * gram_bn, penalty[2])
    return (factor_a_new, dual_a_new, factor_b_new, dual_b_new, factor_c_new, dual_c_new)
```

```python
import functools

import jax
import jax.numpy as jnp
from jax import lax
from jax.experimental import pallas as pl
from jax.experimental.pallas import tpu as pltpu
from jax.sharding import PartitionSpec as P

ITERS = 6
REACH = 2
LANES = 128
MESH_ID = pl.DeviceIdType.MESH
HIGHEST = lax.Precision.HIGHEST
VMEM_SPEC = pl.BlockSpec(memory_space=pltpu.VMEM)
SMEM_SPEC = pl.BlockSpec(memory_space=pltpu.SMEM)
VMEM_BYTES = 56 * 1024 * 1024


def window_offsets():
    offsets = [0]
    for distance in range(1, REACH + 1):
        offsets.append(distance)
        offsets.append(-distance)
    return offsets


OFFSETS = window_offsets()


def block_pairs(rank):
    count = rank // LANES
    return [(i, j) for i in range(count) for j in range(i, count)]


def packed_rows(rank, matrices, devices):
    unit = 8 * devices
    return -(-matrices * len(block_pairs(rank)) * LANES // unit) * unit


def f32_dot(left, right):
    return jnp.dot(left, right, precision=HIGHEST, preferred_element_type=jnp.float32)


def bf_dot(left, right):
    return jnp.dot(left, right, preferred_element_type=jnp.float32)


def write_gram(out_ref, start, factor):
    rank = factor.shape[1]
    turned = factor.T
    place = start
    for i in range(rank // LANES):
        band = f32_dot(turned[i * LANES : (i + 1) * LANES, :], factor[:, i * LANES :])
        for j in range(i, rank // LANES):
            out_ref[place : place + LANES, :] = band[:, (j - i) * LANES : (j - i + 1) * LANES]
            place += LANES
    return place


def gram_pair_kernel(b_ref, c_ref, gram_ref, low_b_ref, low_c_ref):
    place = write_gram(gram_ref, 0, b_ref[0])
    place = write_gram(gram_ref, place, c_ref[0])
    if place < gram_ref.shape[0]:
        gram_ref[place:, :] = jnp.zeros((gram_ref.shape[0] - place, LANES), jnp.float32)
    low_b_ref[...] = b_ref[0].astype(jnp.bfloat16)
    low_c_ref[...] = c_ref[0].astype(jnp.bfloat16)


def greet(devices, me, with_cube):
    others = []
    if with_cube:
        for t in range(devices.bit_length() - 1):
            bit = (me // (1 << t)) % 2
            others.append(me + (1 - 2 * bit) * (1 << t))
    for offset in OFFSETS[1:]:
        others.append((me + offset + devices) % devices)
    barrier = pltpu.get_barrier_semaphore()
    for other in others:
        pl.semaphore_signal(barrier, inc=1, device_id=(other,), device_id_type=MESH_ID)
    pl.semaphore_wait(barrier, len(others))


def share_kernel(devices, payloads, *refs):
    gram_ref = refs[0]
    own_refs = refs[1 : 1 + payloads]
    sum_ref = refs[1 + payloads]
    win_refs = refs[2 + payloads : 2 + 2 * payloads]
    box_ref, part_ref, win_send, win_recv, local_sem, cube_send, cube_recv = refs[2 + 2 * payloads :]
    me = lax.axis_index("dev")
    greet(devices, me, True)
    window_copies = []
    for place in range(1, len(OFFSETS)):
        target = (me - OFFSETS[place] + devices) % devices
        for q in range(payloads):
            copy = pltpu.make_async_remote_copy(
                src_ref=own_refs[q],
                dst_ref=win_refs[q].at[place],
                send_sem=win_send.at[q, place],
                recv_sem=win_recv.at[q, place],
                device_id=(target,),
                device_id_type=MESH_ID,
            )
            copy.start()
            window_copies.append(copy)
    for q in range(payloads):
        own = pltpu.make_async_copy(own_refs[q], win_refs[q].at[0], local_sem.at[q])
        own.start()
        window_copies.append(own)

    steps = devices.bit_length() - 1
    length = gram_ref.shape[0]
    start = 0
    box = 0
    for t in range(steps):
        half = length // 2
        bit = (me // (1 << t)) % 2
        partner = me + (1 - 2 * bit) * (1 << t)
        keep = pl.multiple_of(start + bit * half, 8)
        give = pl.multiple_of(start + (1 - bit) * half, 8)
        source = gram_ref if t == 0 else part_ref
        target = sum_ref if t == steps - 1 else part_ref
        copy = pltpu.make_async_remote_copy(
            src_ref=source.at[pl.ds(give, half)],
            dst_ref=box_ref.at[pl.ds(box, half)],
            send_sem=cube_send.at[t],
            recv_sem=cube_recv.at[t],
            device_id=(partner,),
            device_id_type=MESH_ID,
        )
        copy.start()
        copy.wait()
        target[pl.ds(keep, half), :] = source[pl.ds(keep, half), :] + box_ref[pl.ds(box, half), :]
        box += half
        start = keep
        length = half
    for t in reversed(range(steps)):
        bit = (me // (1 << t)) % 2
        partner = me + (1 - 2 * bit) * (1 << t)
        piece = pl.ds(pl.multiple_of(start, 8), length)
        copy = pltpu.make_async_remote_copy(
            src_ref=sum_ref.at[piece],
            dst_ref=sum_ref.at[piece],
            send_sem=cube_send.at[steps + t],
            recv_sem=cube_recv.at[steps + t],
            device_id=(partner,),
            device_id_type=MESH_ID,
        )
        copy.start()
        copy.wait()
        start = start - bit * length
        length = 2 * length
    for copy in window_copies:
        copy.wait()


def share(devices, call_id, gram, payload):
    steps = devices.bit_length() - 1
    win = len(OFFSETS)
    count = len(payload)
    result = pl.pallas_call(
        functools.partial(share_kernel, devices, count),
        out_shape=[jax.ShapeDtypeStruct(gram.shape, jnp.float32)]
        + [jax.ShapeDtypeStruct((win,) + p.shape, p.dtype) for p in payload],
        in_specs=[VMEM_SPEC] * (1 + count),
        out_specs=[VMEM_SPEC] * (1 + count),
        scratch_shapes=[
            pltpu.VMEM(gram.shape, jnp.float32),
            pltpu.VMEM(gram.shape, jnp.float32),
            pltpu.SemaphoreType.DMA((count, win)),
            pltpu.SemaphoreType.DMA((count, win)),
            pltpu.SemaphoreType.DMA((count,)),
            pltpu.SemaphoreType.DMA((2 * steps,)),
            pltpu.SemaphoreType.DMA((2 * steps,)),
        ],
        compiler_params=pltpu.CompilerParams(
            collective_id=call_id, has_side_effects=True, vmem_limit_bytes=VMEM_BYTES
        ),
        name=f"share_{call_id}",
    )(gram, *payload)
    return result[0], result[1:]


def fold_kernel(devices, totals_ref, out_ref, box_ref, send_sem, recv_sem):
    me = lax.axis_index("dev")
    greet(devices, me, False)
    copies = []
    for place in range(1, len(OFFSETS)):
        copy = pltpu.make_async_remote_copy(
            src_ref=totals_ref.at[place],
            dst_ref=box_ref.at[place],
            send_sem=send_sem.at[place],
            recv_sem=recv_sem.at[place],
            device_id=((me + OFFSETS[place] + devices) % devices,),
            device_id_type=MESH_ID,
        )
        copy.start()
        copies.append(copy)
    for copy in copies:
        copy.wait()
    total = totals_ref[0]
    for place in range(1, len(OFFSETS)):
        total = total + box_ref[place]
    out_ref[...] = total


def fold(devices, call_id, totals):
    win = len(OFFSETS)
    return pl.pallas_call(
        functools.partial(fold_kernel, devices),
        out_shape=jax.ShapeDtypeStruct(totals.shape[1:], jnp.float32),
        in_specs=[VMEM_SPEC],
        out_specs=VMEM_SPEC,
        scratch_shapes=[
            pltpu.VMEM(totals.shape, jnp.float32),
            pltpu.SemaphoreType.DMA((win,)),
            pltpu.SemaphoreType.DMA((win,)),
        ],
        compiler_params=pltpu.CompilerParams(
            collective_id=call_id, has_side_effects=True, vmem_limit_bytes=VMEM_BYTES
        ),
        name=f"fold_{call_id}",
    )(totals)


def tile_kernel(mode, pos_ref, count_ref, tile_ref, left_ref, right_ref, out_ref, acc_ref):
    slot = pl.program_id(0)
    rows_first, rows_second, rows_third = tile_ref.shape[1:]
    rank = out_ref.shape[2]

    @pl.when(slot == 0)
    def _():
        out_ref[...] = jnp.zeros_like(out_ref)

    @pl.when(slot < count_ref[0])
    def _():
        at_left = pos_ref[slot, 0 if mode else 1]
        at_right = pos_ref[slot, 1 if mode == 2 else 2]
        for part in range(rank // LANES):
            lanes = slice(part * LANES, (part + 1) * LANES)
            right = right_ref[at_right, :, lanes]
            if mode == 0:
                left = left_ref[at_left, :, lanes].astype(jnp.float32)

                def row_step(group, carry):
                    base = pl.multiple_of(group * 8, 8)
                    sums = []
                    for i in range(8):
                        product = bf_dot(tile_ref[0, base + i], right)
                        sums.append(jnp.sum(product * left, axis=0, keepdims=True))
                    acc_ref[pl.ds(base, 8), lanes] = jnp.concatenate(sums, axis=0)
                    return carry

                lax.fori_loop(0, rows_first // 8, row_step, 0)
            else:
                acc_ref[0:rows_first, lanes] = left_ref[at_left, :, lanes].astype(jnp.float32)

                def row_add(group, total):
                    base = pl.multiple_of(group * 8, 8)
                    weights = acc_ref[pl.ds(base, 8), lanes]
                    for i in range(8):
                        if mode == 1:
                            product = bf_dot(tile_ref[0, base + i], right)
                        else:
                            product = lax.dot_general(
                                tile_ref[0, base + i],
                                right,
                                (((0,), (0,)), ((), ())),
                                preferred_element_type=jnp.float32,
                            )
                        total = total + product * weights[i : i + 1, :]
                    return total

                rows_out = rows_second if mode == 1 else rows_third
                total = lax.fori_loop(
                    0, rows_first // 8, row_add, jnp.zeros((rows_out, LANES), jnp.float32)
                )
                at_out = pos_ref[slot, mode]
                out_ref[at_out, :, lanes] += total
        if mode == 0:
            out_ref[pos_ref[slot, 0]] += acc_ref[...]


def tile_products(mode, positions, count, tiles, left, right):
    slots, rows_first, rows_second, rows_third = tiles.shape
    rank = left.shape[2]
    win = len(OFFSETS)
    rows_out = (rows_first, rows_second, rows_third)[mode]
    whole = lambda s, pos, cnt: (0, 0, 0)
    live = lambda s, pos, cnt: (jnp.minimum(s, cnt[0] - 1), 0, 0, 0)
    flops = 2 * tiles.size * rank
    return pl.pallas_call(
        functools.partial(tile_kernel, mode),
        out_shape=jax.ShapeDtypeStruct((win, rows_out, rank), jnp.float32),
        grid_spec=pltpu.PrefetchScalarGridSpec(
            num_scalar_prefetch=2,
            grid=(slots,),
            in_specs=[
                pl.BlockSpec((1, rows_first, rows_second, rows_third), live),
                pl.BlockSpec(left.shape, whole),
                pl.BlockSpec(right.shape, whole),
            ],
            out_specs=pl.BlockSpec((win, rows_out, rank), whole),
            scratch_shapes=[pltpu.VMEM((rows_first, rank), jnp.float32)],
        ),
        compiler_params=pltpu.CompilerParams(
            dimension_semantics=("arbitrary",), vmem_limit_bytes=VMEM_BYTES
        ),
        cost_estimate=pl.CostEstimate(
            flops=flops, bytes_accessed=2 * tiles.size, transcendentals=0
        ),
        name=f"tiles_{mode}",
    )(positions, count, tiles, left, right)


def split(value):
    high = value.astype(jnp.bfloat16)
    low = (value - high.astype(jnp.float32)).astype(jnp.bfloat16)
    return high, low


def admm_kernel(mode, starts, last, *refs):
    p1_ref, p2_ref, m_ref, h_ref, u_ref, weight_ref, h_out, u_out = refs[:8]
    if last:
        low_out = gram_out = None
        rest = refs[8:]
    else:
        low_out, gram_out = refs[8:10]
        rest = refs[10:]
    a_ref, x_ref, a_hi, a_lo, x_hi, x_lo, y_hi, y_lo = rest
    rank = h_ref.shape[2]
    weight = weight_ref[mode]
    block_rows = lax.broadcasted_iota(jnp.int32, (LANES, LANES), 0)
    block_cols = lax.broadcasted_iota(jnp.int32, (LANES, LANES), 1)
    on_diag = block_rows == block_cols
    trace = jnp.zeros((), jnp.float32)
    for index, (i, j) in enumerate(block_pairs(rank)):
        row = index * LANES
        one = p1_ref[starts[0] + row : starts[0] + row + LANES, :]
        two = p2_ref[starts[1] + row : starts[1] + row + LANES, :]
        block = one * two
        a_ref[i * LANES : (i + 1) * LANES, j * LANES : (j + 1) * LANES] = block
        if i == j:
            trace = trace + jnp.sum(jnp.where(on_diag, block, 0.0))
        else:
            a_ref[j * LANES : (j + 1) * LANES, i * LANES : (i + 1) * LANES] = block.T
    mean = trace / rank
    rho = weight * mean
    top = trace + rho
    low_end = weight / (rank + weight)
    scale = jnp.minimum(2.0 / (1.0 + low_end), 1.95)
    first = scale / top
    rows = lax.broadcasted_iota(jnp.int32, (LANES, rank), 0)
    cols = lax.broadcasted_iota(jnp.int32, (LANES, rank), 1)
    for i in range(rank // LANES):
        band = slice(i * LANES, (i + 1) * LANES)
        diag = rows + i * LANES == cols
        a = a_ref[band, :] + jnp.where(diag, rho, 0.0)
        a_ref[band, :] = a
        a_hi[band, :], a_lo[band, :] = split(a)
        x_ref[band, :] = jnp.where(diag, 2.0 * first, 0.0) - (first * first) * a

    def ends(low, scale):
        return jnp.minimum(scale * low * (2.0 - scale * low), scale * (2.0 - scale))

    def sweep(index, low):
        scale = jnp.minimum(2.0 / (1.0 + low), 1.95)
        for i in range(rank // LANES):
            band = slice(i * LANES, (i + 1) * LANES)
            x = x_ref[band, :] * scale
            x_ref[band, :] = x
            x_hi[band, :], x_lo[band, :] = split(x)
        for i in range(2):
            band = slice(i * (rank // 2), (i + 1) * (rank // 2))
            xh = x_hi[band, :]
            y = bf_dot(xh, a_hi[...]) + (bf_dot(xh, a_lo[...]) + bf_dot(x_lo[band, :], a_hi[...]))
            y_hi[band, :], y_lo[band, :] = split(y)
        for i in range(2):
            band = slice(i * (rank // 2), (i + 1) * (rank // 2))
            yh = y_hi[band, :]
            z = bf_dot(yh, x_hi[...]) + (bf_dot(yh, x_lo[...]) + bf_dot(y_lo[band, :], x_hi[...]))
            x_ref[band, :] = 2.0 * x_ref[band, :] - z
        return ends(low, scale)

    lax.fori_loop(0, 6, sweep, ends(low_end, scale))
    for i in range(rank // LANES):
        band = slice(i * LANES, (i + 1) * LANES)
        x_hi[band, :], x_lo[band, :] = split(x_ref[band, :])
        diag = rows + i * LANES == cols
        rest_of = jnp.where(diag, 1.0, 0.0) - f32_dot(x_ref[band, :], a_ref[...])
        y_hi[band, :] = rest_of.astype(jnp.bfloat16)
    x_ref[...] = x_ref[...] + bf_dot(y_hi[...], x_hi[...])

    mttkrp = m_ref[...]
    factor = h_ref[0]
    dual = u_ref[0]
    for sweep_index in range(ITERS):
        auxiliary = f32_dot(mttkrp + rho * (factor + dual), x_ref[...])
        factor = jnp.maximum(auxiliary - dual, 0.0)
        dual = dual + factor - auxiliary
    h_out[0] = factor
    u_out[0] = dual
    if not last:
        low_out[...] = factor.astype(jnp.bfloat16)
        place = write_gram(gram_out, 0, factor)
        if place < gram_out.shape[0]:
            gram_out[place:, :] = jnp.zeros((gram_out.shape[0] - place, LANES), jnp.float32)


def admm(mode, devices, packed, starts, mttkrp, factor, dual, penalty, last):
    rank = factor.shape[2]
    square = (rank, rank)
    out_shape = [
        jax.ShapeDtypeStruct(factor.shape, jnp.float32),
        jax.ShapeDtypeStruct(factor.shape, jnp.float32),
    ]
    if not last:
        out_shape += [
            jax.ShapeDtypeStruct(factor.shape[1:], jnp.bfloat16),
            jax.ShapeDtypeStruct((packed_rows(rank, 1, devices), LANES), jnp.float32),
        ]
    return pl.pallas_call(
        functools.partial(admm_kernel, mode, starts, last),
        out_shape=out_shape,
        in_specs=[VMEM_SPEC] * 5 + [SMEM_SPEC],
        out_specs=[VMEM_SPEC] * len(out_shape),
        scratch_shapes=[pltpu.VMEM(square, jnp.float32)] * 2
        + [pltpu.VMEM(square, jnp.bfloat16)] * 6,
        compiler_params=pltpu.CompilerParams(vmem_limit_bytes=VMEM_BYTES),
        name=f"admm_{mode}",
    )(packed[0], packed[1], mttkrp, factor, dual, penalty)


def per_device(
    devices,
    tensor_tiles,
    tile_coords,
    tile_count,
    owned_i,
    owned_j,
    owned_k,
    factor_a,
    factor_b,
    factor_c,
    dual_a,
    dual_b,
    dual_c,
    penalty,
):
    rank = factor_a.shape[2]
    one_gram = len(block_pairs(rank)) * LANES
    own_ids = jnp.broadcast_to(
        jnp.concatenate([owned_i, owned_j, owned_k, jnp.zeros((5,), jnp.int32)])[:, None],
        (8, LANES),
    )
    gram_bc, low_b, low_c = pl.pallas_call(
        gram_pair_kernel,
        out_shape=[
            jax.ShapeDtypeStruct((packed_rows(rank, 2, devices), LANES), jnp.float32),
            jax.ShapeDtypeStruct(factor_b.shape[1:], jnp.bfloat16),
            jax.ShapeDtypeStruct(factor_c.shape[1:], jnp.bfloat16),
        ],
        in_specs=[VMEM_SPEC] * 2,
        out_specs=[VMEM_SPEC] * 3,
        compiler_params=pltpu.CompilerParams(vmem_limit_bytes=VMEM_BYTES),
        name="gram_pair",
    )(factor_b, factor_c)
    gram_bc, (win_b, win_c, ids) = share(devices, 0, gram_bc, (low_b, low_c, own_ids))
    window_ids = ids[:, :3, 0]
    match = tile_coords[:, None, :] == window_ids[None, :, :]
    places = jnp.arange(len(OFFSETS), dtype=jnp.int32)[None, :, None]
    positions = jnp.sum(jnp.where(match, places, 0), axis=1)
    positions = jnp.minimum(positions, len(OFFSETS) - 1)

    totals = tile_products(0, positions, tile_count, tensor_tiles, win_b, win_c)
    mttkrp_a = fold(devices, 3, totals)
    factor_a_new, dual_a_new, low_a, gram_a = admm(
        0, devices, (gram_bc, gram_bc), (0, one_gram), mttkrp_a, factor_a, dual_a, penalty, False
    )
    gram_a, (win_a,) = share(devices, 1, gram_a, (low_a,))

    totals = tile_products(1, positions, tile_count, tensor_tiles, win_a, win_c)
    mttkrp_b = fold(devices, 4, totals)
    factor_b_new, dual_b_new, low_bn, gram_bn = admm(
        1, devices, (gram_a, gram_bc), (0, one_gram), mttkrp_b, factor_b, dual_b, penalty, False
    )
    gram_bn, (win_bn,) = share(devices, 2, gram_bn, (low_bn,))

    totals = tile_products(2, positions, tile_count, tensor_tiles, win_a, win_bn)
    mttkrp_c = fold(devices, 5, totals)
    factor_c_new, dual_c_new = admm(
        2, devices, (gram_a, gram_bn), (0, 0), mttkrp_c, factor_c, dual_c, penalty, True
    )
    return (factor_a_new, dual_a_new, factor_b_new, dual_b_new, factor_c_new, dual_c_new)


def solution(mesh):
    block = P("dev", None, None)
    return jax.shard_map(
        functools.partial(per_device, mesh.shape["dev"]),
        mesh=mesh,
        in_specs=(
            P("dev", None, None, None),
            P("dev", None),
            P("dev"),
            P("dev"),
            P("dev"),
            P("dev"),
            block,
            block,
            block,
            block,
            block,
            block,
            P(),
        ),
        out_specs=(block,) * 6,
        check_vma=False,
    )
```

```python
import functools

import jax
import jax.numpy as jnp
from jax import lax
from jax.experimental import pallas as pl
from jax.experimental.pallas import tpu as pltpu
from jax.sharding import PartitionSpec as P

ITERS = 6
REACH = 2
LANES = 128
WIDE = 256
MESH_ID = pl.DeviceIdType.MESH
HIGHEST = lax.Precision.HIGHEST
VMEM_SPEC = pl.BlockSpec(memory_space=pltpu.VMEM)
SMEM_SPEC = pl.BlockSpec(memory_space=pltpu.SMEM)
VMEM_BYTES = 56 * 1024 * 1024


def window_offsets():
    offsets = [0]
    for distance in range(1, REACH + 1):
        offsets.append(distance)
        offsets.append(-distance)
    return offsets


OFFSETS = window_offsets()


def block_pairs(rank):
    count = rank // LANES
    return [(i, j) for i in range(count) for j in range(i, count)]


def packed_rows(rank, matrices, devices):
    unit = 8 * devices
    return -(-matrices * len(block_pairs(rank)) * LANES // unit) * unit


def f32_dot(left, right):
    return jnp.dot(left, right, precision=HIGHEST, preferred_element_type=jnp.float32)


def bf_dot(left, right):
    return jnp.dot(left, right, preferred_element_type=jnp.float32)


def write_gram(out_ref, start, factor):
    rank = factor.shape[1]
    turned = factor.T
    place = start
    for i in range(rank // LANES):
        band = f32_dot(turned[i * LANES : (i + 1) * LANES, :], factor[:, i * LANES :])
        for j in range(i, rank // LANES):
            out_ref[place : place + LANES, :] = band[:, (j - i) * LANES : (j - i + 1) * LANES]
            place += LANES
    return place


def gram_pair_kernel(b_ref, c_ref, gram_ref, low_b_ref, low_c_ref):
    place = write_gram(gram_ref, 0, b_ref[0])
    place = write_gram(gram_ref, place, c_ref[0])
    if place < gram_ref.shape[0]:
        gram_ref[place:, :] = jnp.zeros((gram_ref.shape[0] - place, LANES), jnp.float32)
    low_b_ref[...] = b_ref[0].astype(jnp.bfloat16)
    low_c_ref[...] = c_ref[0].astype(jnp.bfloat16)


def cube_levels(devices):
    levels = []
    stride = 1
    while stride < devices:
        radix = 2 if stride == 1 or devices // stride % 4 else 4
        levels.append((radix, stride))
        stride *= radix
    return levels


def greet(devices, me, with_cube):
    others = []
    if with_cube:
        for radix, stride in cube_levels(devices):
            digit = (me // stride) % radix
            for turn in range(1, radix):
                others.append(me + ((digit + turn) % radix - digit) * stride)
    for offset in OFFSETS[1:]:
        others.append((me + offset + devices) % devices)
    barrier = pltpu.get_barrier_semaphore()
    for other in others:
        pl.semaphore_signal(barrier, inc=1, device_id=(other,), device_id_type=MESH_ID)
    pl.semaphore_wait(barrier, len(others))


def share_kernel(devices, payloads, *refs):
    gram_ref = refs[0]
    own_refs = refs[1 : 1 + payloads]
    sum_ref = refs[1 + payloads]
    win_refs = refs[2 + payloads : 2 + 2 * payloads]
    box_ref, part_ref, win_send, win_recv, local_sem, cube_send, cube_recv = refs[2 + 2 * payloads :]
    me = lax.axis_index("dev")
    greet(devices, me, True)
    levels = cube_levels(devices)
    length = gram_ref.shape[0]
    start = 0
    box = 0
    window_copies = []
    for level, (radix, stride) in enumerate(levels):
        piece = length // radix
        digit = (me // stride) % radix
        source = gram_ref if level == 0 else part_ref
        target = sum_ref if level == len(levels) - 1 else part_ref
        copies = []
        for turn in range(1, radix):
            other = (digit + turn) % radix
            give = pl.multiple_of(start + other * piece, 8)
            copy = pltpu.make_async_remote_copy(
                src_ref=source.at[pl.ds(give, piece)],
                dst_ref=box_ref.at[pl.ds(box + (turn - 1) * piece, piece)],
                send_sem=cube_send.at[level, turn],
                recv_sem=cube_recv.at[level, turn],
                device_id=(me + (other - digit) * stride,),
                device_id_type=MESH_ID,
            )
            copy.start()
            copies.append(copy)
        if level == 0:
            for place in range(1, len(OFFSETS)):
                window_to = (me - OFFSETS[place] + devices) % devices
                for q in range(payloads):
                    copy = pltpu.make_async_remote_copy(
                        src_ref=own_refs[q],
                        dst_ref=win_refs[q].at[place],
                        send_sem=win_send.at[q, place],
                        recv_sem=win_recv.at[q, place],
                        device_id=(window_to,),
                        device_id_type=MESH_ID,
                    )
                    copy.start()
                    window_copies.append(copy)
            for q in range(payloads):
                own = pltpu.make_async_copy(own_refs[q], win_refs[q].at[0], local_sem.at[q])
                own.start()
                window_copies.append(own)
        for copy in copies:
            copy.wait()
        keep = pl.multiple_of(start + digit * piece, 8)
        total = source[pl.ds(keep, piece), :]
        for turn in range(1, radix):
            total = total + box_ref[box + (turn - 1) * piece : box + turn * piece, :]
        target[pl.ds(keep, piece), :] = total
        box += (radix - 1) * piece
        start = keep
        length = piece
    for level in reversed(range(len(levels))):
        radix, stride = levels[level]
        digit = (me // stride) % radix
        piece = pl.ds(pl.multiple_of(start, 8), length)
        copies = []
        for turn in range(1, radix):
            other = (digit + turn) % radix
            copy = pltpu.make_async_remote_copy(
                src_ref=sum_ref.at[piece],
                dst_ref=sum_ref.at[piece],
                send_sem=cube_send.at[len(levels) + level, turn],
                recv_sem=cube_recv.at[len(levels) + level, turn],
                device_id=(me + (other - digit) * stride,),
                device_id_type=MESH_ID,
            )
            copy.start()
            copies.append(copy)
        for copy in copies:
            copy.wait()
        start = start - digit * length
        length = radix * length
    for copy in window_copies:
        copy.wait()


def share(devices, call_id, gram, payload):
    phases = 2 * len(cube_levels(devices))
    win = len(OFFSETS)
    count = len(payload)
    result = pl.pallas_call(
        functools.partial(share_kernel, devices, count),
        out_shape=[jax.ShapeDtypeStruct(gram.shape, jnp.float32)]
        + [jax.ShapeDtypeStruct((win,) + p.shape, p.dtype) for p in payload],
        in_specs=[VMEM_SPEC] * (1 + count),
        out_specs=[VMEM_SPEC] * (1 + count),
        scratch_shapes=[
            pltpu.VMEM(gram.shape, jnp.float32),
            pltpu.VMEM(gram.shape, jnp.float32),
            pltpu.SemaphoreType.DMA((count, win)),
            pltpu.SemaphoreType.DMA((count, win)),
            pltpu.SemaphoreType.DMA((count,)),
            pltpu.SemaphoreType.DMA((phases, 4)),
            pltpu.SemaphoreType.DMA((phases, 4)),
        ],
        compiler_params=pltpu.CompilerParams(
            collective_id=call_id, has_side_effects=True, vmem_limit_bytes=VMEM_BYTES
        ),
        name=f"share_{call_id}",
    )(gram, *payload)
    return result[0], result[1:]


def fold_kernel(devices, totals_ref, out_ref, box_ref, send_sem, recv_sem):
    me = lax.axis_index("dev")
    greet(devices, me, False)
    copies = []
    for place in range(1, len(OFFSETS)):
        copy = pltpu.make_async_remote_copy(
            src_ref=totals_ref.at[place],
            dst_ref=box_ref.at[place],
            send_sem=send_sem.at[place],
            recv_sem=recv_sem.at[place],
            device_id=((me + OFFSETS[place] + devices) % devices,),
            device_id_type=MESH_ID,
        )
        copy.start()
        copies.append(copy)
    for copy in copies:
        copy.wait()
    total = totals_ref[0]
    for place in range(1, len(OFFSETS)):
        total = total + box_ref[place]
    out_ref[...] = total


def fold(devices, call_id, totals):
    win = len(OFFSETS)
    return pl.pallas_call(
        functools.partial(fold_kernel, devices),
        out_shape=jax.ShapeDtypeStruct(totals.shape[1:], jnp.float32),
        in_specs=[VMEM_SPEC],
        out_specs=VMEM_SPEC,
        scratch_shapes=[
            pltpu.VMEM(totals.shape, jnp.float32),
            pltpu.SemaphoreType.DMA((win,)),
            pltpu.SemaphoreType.DMA((win,)),
        ],
        compiler_params=pltpu.CompilerParams(
            collective_id=call_id, has_side_effects=True, vmem_limit_bytes=VMEM_BYTES
        ),
        name=f"fold_{call_id}",
    )(totals)


def tile_kernel(mode, pos_ref, count_ref, tile_ref, left_ref, right_ref, out_ref, acc_ref):
    slot = pl.program_id(0)
    rows_first, rows_second, rows_third = tile_ref.shape[1:]
    rank = out_ref.shape[2]

    @pl.when(slot == 0)
    def _():
        out_ref[...] = jnp.zeros_like(out_ref)

    @pl.when(slot < count_ref[0])
    def _():
        at_left = pos_ref[slot, 0 if mode else 1]
        at_right = pos_ref[slot, 1 if mode == 2 else 2]
        wide = min(WIDE, rank)
        for part in range(rank // wide):
            lanes = slice(part * wide, (part + 1) * wide)
            right = right_ref[at_right, :, lanes]
            if mode == 0:
                left = left_ref[at_left, :, lanes].astype(jnp.float32)

                def row_step(group, carry):
                    base = pl.multiple_of(group * 8, 8)
                    sums = []
                    for i in range(8):
                        product = bf_dot(tile_ref[0, base + i], right)
                        sums.append(jnp.sum(product * left, axis=0, keepdims=True))
                    acc_ref[pl.ds(base, 8), lanes] = jnp.concatenate(sums, axis=0)
                    return carry

                lax.fori_loop(0, rows_first // 8, row_step, 0)
            else:
                acc_ref[0:rows_first, lanes] = left_ref[at_left, :, lanes].astype(jnp.float32)

                def row_add(group, total):
                    base = pl.multiple_of(group * 8, 8)
                    weights = acc_ref[pl.ds(base, 8), lanes]
                    for i in range(8):
                        if mode == 1:
                            product = bf_dot(tile_ref[0, base + i], right)
                        else:
                            product = lax.dot_general(
                                tile_ref[0, base + i],
                                right,
                                (((0,), (0,)), ((), ())),
                                preferred_element_type=jnp.float32,
                            )
                        total = total + product * weights[i : i + 1, :]
                    return total

                rows_out = rows_second if mode == 1 else rows_third
                total = lax.fori_loop(
                    0, rows_first // 8, row_add, jnp.zeros((rows_out, wide), jnp.float32)
                )
                at_out = pos_ref[slot, mode]
                out_ref[at_out, :, lanes] += total
        if mode == 0:
            out_ref[pos_ref[slot, 0]] += acc_ref[...]


def tile_products(mode, positions, count, tiles, left, right):
    slots, rows_first, rows_second, rows_third = tiles.shape
    rank = left.shape[2]
    win = len(OFFSETS)
    rows_out = (rows_first, rows_second, rows_third)[mode]
    whole = lambda s, pos, cnt: (0, 0, 0)
    live = lambda s, pos, cnt: (jnp.minimum(s, cnt[0] - 1), 0, 0, 0)
    flops = 2 * tiles.size * rank
    return pl.pallas_call(
        functools.partial(tile_kernel, mode),
        out_shape=jax.ShapeDtypeStruct((win, rows_out, rank), jnp.float32),
        grid_spec=pltpu.PrefetchScalarGridSpec(
            num_scalar_prefetch=2,
            grid=(slots,),
            in_specs=[
                pl.BlockSpec((1, rows_first, rows_second, rows_third), live),
                pl.BlockSpec(left.shape, whole),
                pl.BlockSpec(right.shape, whole),
            ],
            out_specs=pl.BlockSpec((win, rows_out, rank), whole),
            scratch_shapes=[pltpu.VMEM((rows_first, rank), jnp.float32)],
        ),
        compiler_params=pltpu.CompilerParams(
            dimension_semantics=("arbitrary",), vmem_limit_bytes=VMEM_BYTES
        ),
        cost_estimate=pl.CostEstimate(
            flops=flops, bytes_accessed=2 * tiles.size, transcendentals=0
        ),
        name=f"tiles_{mode}",
    )(positions, count, tiles, left, right)


def split(value):
    high = value.astype(jnp.bfloat16)
    low = (value - high.astype(jnp.float32)).astype(jnp.bfloat16)
    return high, low


def admm_kernel(mode, starts, last, *refs):
    p1_ref, p2_ref, m_ref, h_ref, u_ref, weight_ref, h_out, u_out = refs[:8]
    if last:
        low_out = gram_out = None
        rest = refs[8:]
    else:
        low_out, gram_out = refs[8:10]
        rest = refs[10:]
    a_ref, x_ref, a_hi, a_lo, x_hi, x_lo, y_hi, y_lo = rest
    rank = h_ref.shape[2]
    weight = weight_ref[mode]
    block_rows = lax.broadcasted_iota(jnp.int32, (LANES, LANES), 0)
    block_cols = lax.broadcasted_iota(jnp.int32, (LANES, LANES), 1)
    on_diag = block_rows == block_cols
    trace = jnp.zeros((), jnp.float32)
    for index, (i, j) in enumerate(block_pairs(rank)):
        row = index * LANES
        one = p1_ref[starts[0] + row : starts[0] + row + LANES, :]
        two = p2_ref[starts[1] + row : starts[1] + row + LANES, :]
        block = one * two
        a_ref[i * LANES : (i + 1) * LANES, j * LANES : (j + 1) * LANES] = block
        if i == j:
            trace = trace + jnp.sum(jnp.where(on_diag, block, 0.0))
        else:
            a_ref[j * LANES : (j + 1) * LANES, i * LANES : (i + 1) * LANES] = block.T
    mean = trace / rank
    rho = weight * mean
    top = trace + rho
    low_end = weight / (rank + weight)
    scale = jnp.minimum(2.0 / (1.0 + low_end), 1.95)
    first = scale / top
    rows = lax.broadcasted_iota(jnp.int32, (LANES, rank), 0)
    cols = lax.broadcasted_iota(jnp.int32, (LANES, rank), 1)
    for i in range(rank // LANES):
        band = slice(i * LANES, (i + 1) * LANES)
        diag = rows + i * LANES == cols
        a = a_ref[band, :] + jnp.where(diag, rho, 0.0)
        a_ref[band, :] = a
        a_hi[band, :], a_lo[band, :] = split(a)
        x_ref[band, :] = jnp.where(diag, 2.0 * first, 0.0) - (first * first) * a

    def ends(low, scale):
        return jnp.minimum(scale * low * (2.0 - scale * low), scale * (2.0 - scale))

    def sweep(index, low):
        scale = jnp.minimum(2.0 / (1.0 + low), 1.95)
        for i in range(rank // LANES):
            band = slice(i * LANES, (i + 1) * LANES)
            x = x_ref[band, :] * scale
            x_ref[band, :] = x
            x_hi[band, :], x_lo[band, :] = split(x)
        for i in range(2):
            band = slice(i * (rank // 2), (i + 1) * (rank // 2))
            xh = x_hi[band, :]
            y = bf_dot(xh, a_hi[...]) + (bf_dot(xh, a_lo[...]) + bf_dot(x_lo[band, :], a_hi[...]))
            y_hi[band, :], y_lo[band, :] = split(y)
        for i in range(2):
            band = slice(i * (rank // 2), (i + 1) * (rank // 2))
            yh = y_hi[band, :]
            z = bf_dot(yh, x_hi[...]) + (bf_dot(yh, x_lo[...]) + bf_dot(y_lo[band, :], x_hi[...]))
            x_ref[band, :] = 2.0 * x_ref[band, :] - z
        return ends(low, scale)

    lax.fori_loop(0, 6, sweep, ends(low_end, scale))
    for i in range(rank // LANES):
        band = slice(i * LANES, (i + 1) * LANES)
        x_hi[band, :], x_lo[band, :] = split(x_ref[band, :])
        diag = rows + i * LANES == cols
        rest_of = jnp.where(diag, 1.0, 0.0) - f32_dot(x_ref[band, :], a_ref[...])
        y_hi[band, :] = rest_of.astype(jnp.bfloat16)
    x_ref[...] = x_ref[...] + bf_dot(y_hi[...], x_hi[...])

    mttkrp = m_ref[...]
    factor = h_ref[0]
    dual = u_ref[0]
    for sweep_index in range(ITERS):
        auxiliary = f32_dot(mttkrp + rho * (factor + dual), x_ref[...])
        factor = jnp.maximum(auxiliary - dual, 0.0)
        dual = dual + factor - auxiliary
    h_out[0] = factor
    u_out[0] = dual
    if not last:
        low_out[...] = factor.astype(jnp.bfloat16)
        place = write_gram(gram_out, 0, factor)
        if place < gram_out.shape[0]:
            gram_out[place:, :] = jnp.zeros((gram_out.shape[0] - place, LANES), jnp.float32)


def admm(mode, devices, packed, starts, mttkrp, factor, dual, penalty, last):
    rank = factor.shape[2]
    square = (rank, rank)
    out_shape = [
        jax.ShapeDtypeStruct(factor.shape, jnp.float32),
        jax.ShapeDtypeStruct(factor.shape, jnp.float32),
    ]
    if not last:
        out_shape += [
            jax.ShapeDtypeStruct(factor.shape[1:], jnp.bfloat16),
            jax.ShapeDtypeStruct((packed_rows(rank, 1, devices), LANES), jnp.float32),
        ]
    return pl.pallas_call(
        functools.partial(admm_kernel, mode, starts, last),
        out_shape=out_shape,
        in_specs=[VMEM_SPEC] * 5 + [SMEM_SPEC],
        out_specs=[VMEM_SPEC] * len(out_shape),
        scratch_shapes=[pltpu.VMEM(square, jnp.float32)] * 2
        + [pltpu.VMEM(square, jnp.bfloat16)] * 6,
        compiler_params=pltpu.CompilerParams(vmem_limit_bytes=VMEM_BYTES),
        name=f"admm_{mode}",
    )(packed[0], packed[1], mttkrp, factor, dual, penalty)


def per_device(
    devices,
    tensor_tiles,
    tile_coords,
    tile_count,
    owned_i,
    owned_j,
    owned_k,
    factor_a,
    factor_b,
    factor_c,
    dual_a,
    dual_b,
    dual_c,
    penalty,
):
    rank = factor_a.shape[2]
    one_gram = len(block_pairs(rank)) * LANES
    own_ids = jnp.broadcast_to(
        jnp.concatenate([owned_i, owned_j, owned_k, jnp.zeros((5,), jnp.int32)])[:, None],
        (8, LANES),
    )
    gram_bc, low_b, low_c = pl.pallas_call(
        gram_pair_kernel,
        out_shape=[
            jax.ShapeDtypeStruct((packed_rows(rank, 2, devices), LANES), jnp.float32),
            jax.ShapeDtypeStruct(factor_b.shape[1:], jnp.bfloat16),
            jax.ShapeDtypeStruct(factor_c.shape[1:], jnp.bfloat16),
        ],
        in_specs=[VMEM_SPEC] * 2,
        out_specs=[VMEM_SPEC] * 3,
        compiler_params=pltpu.CompilerParams(vmem_limit_bytes=VMEM_BYTES),
        name="gram_pair",
    )(factor_b, factor_c)
    gram_bc, (win_b, win_c, ids) = share(devices, 0, gram_bc, (low_b, low_c, own_ids))
    window_ids = ids[:, :3, 0]
    match = tile_coords[:, None, :] == window_ids[None, :, :]
    places = jnp.arange(len(OFFSETS), dtype=jnp.int32)[None, :, None]
    positions = jnp.sum(jnp.where(match, places, 0), axis=1)
    positions = jnp.minimum(positions, len(OFFSETS) - 1)

    totals = tile_products(0, positions, tile_count, tensor_tiles, win_b, win_c)
    mttkrp_a = fold(devices, 3, totals)
    factor_a_new, dual_a_new, low_a, gram_a = admm(
        0, devices, (gram_bc, gram_bc), (0, one_gram), mttkrp_a, factor_a, dual_a, penalty, False
    )
    gram_a, (win_a,) = share(devices, 1, gram_a, (low_a,))

    totals = tile_products(1, positions, tile_count, tensor_tiles, win_a, win_c)
    mttkrp_b = fold(devices, 4, totals)
    factor_b_new, dual_b_new, low_bn, gram_bn = admm(
        1, devices, (gram_a, gram_bc), (0, one_gram), mttkrp_b, factor_b, dual_b, penalty, False
    )
    gram_bn, (win_bn,) = share(devices, 2, gram_bn, (low_bn,))

    totals = tile_products(2, positions, tile_count, tensor_tiles, win_a, win_bn)
    mttkrp_c = fold(devices, 5, totals)
    factor_c_new, dual_c_new = admm(
        2, devices, (gram_a, gram_bn), (0, 0), mttkrp_c, factor_c, dual_c, penalty, True
    )
    return (factor_a_new, dual_a_new, factor_b_new, dual_b_new, factor_c_new, dual_c_new)


def solution(mesh):
    block = P("dev", None, None)
    return jax.shard_map(
        functools.partial(per_device, mesh.shape["dev"]),
        mesh=mesh,
        in_specs=(
            P("dev", None, None, None),
            P("dev", None),
            P("dev"),
            P("dev"),
            P("dev"),
            P("dev"),
            block,
            block,
            block,
            block,
            block,
            block,
            P(),
        ),
        out_specs=(block,) * 6,
        check_vma=False,
    )
```
